128 devices in a mesh: dp: 16 (over x_lo, z, core), shard: 8 (over y, x_hi).
Axes of the slice: x: 4 (x_hi: 2, x_lo: 2; x = x_hi * 2 + x_lo), y: 4, z: 4, core: 2. Of those that a mesh axis runs over, the one named last changes fastest.
Arguments:
- grad_qkv: bfloat16 [16, 768, 2304], P('dp', 'shard'), may hold values from -4 to 4
- grad_out: bfloat16 [16, 768, 768], P('dp', 'shard'), may hold values from -4 to 4
- grad_up: bfloat16 [16, 768, 3072], P('dp', 'shard'), may hold values from -4 to 4
- grad_down: bfloat16 [16, 3072, 768], P('dp', 'shard'), may hold values from -4 to 4
- grad_bias: bfloat16 [16, 9984], P('dp'), may hold values from -6 to 6
- grad_embed: bfloat16 [16, 32768, 768], P('dp', 'shard'), may hold values from -6 to 6
- moment_qkv: float32 [768, 2304], P('shard'), may hold values from -6 to 6
- moment_out: float32 [768, 768], P('shard'), may hold values from -6 to 6
- moment_up: float32 [768, 3072], P('shard'), may hold values from -6 to 6
- moment_down: float32 [3072, 768], P('shard'), may hold values from -6 to 6
- embed_param: float32 [8, 4096, 768], P('shard', 'dp'), may hold values from -6 to 6
- embed_first: float32 [8, 4096, 768], P('shard', 'dp'), may hold values from -6 to 6
- embed_second: float32 [8, 4096, 768], P('shard', 'dp'), may hold values from 0.01 to 1
- bias_param: float32 [9984], replicated, may hold values from -6 to 6
- bias_first: float32 [9984], replicated, may hold values from -6 to 6
- bias_second: float32 [9984], replicated, may hold values from 0.01 to 1
Outputs:
- new_moment_qkv: float32 [768, 2304], P('shard')
- update_qkv: bfloat16 [768, 2304], P('shard')
- new_moment_out: float32 [768, 768], P('shard')
- update_out: bfloat16 [768, 768], P('shard')
- new_moment_up: float32 [768, 3072], P('shard')
- update_up: bfloat16 [768, 3072], P('shard')
- new_moment_down: float32 [3072, 768], P('shard')
- update_down: bfloat16 [3072, 768], P('shard')
- new_embed_param: float32 [8, 4096, 768], P('shard', 'dp')
- new_embed_first: float32 [8, 4096, 768], P('shard', 'dp')
- new_embed_second: float32 [8, 4096, 768], P('shard', 'dp')
- new_bias_param: float32 [9984], replicated
- new_bias_first: float32 [9984], replicated
- new_bias_second: float32 [9984], replicated
The draws below stay inside these ranges and needn't reach their ends.
All inputs are finite; a program needn't handle non-finite values.
Results may differ from the reference program's by a relative error of at most 0.029.
Values may be sent and summed in bfloat16 or wider, within the bound.
A program may use at most 192 MiB of HBM per device.

```python
import math
import jax
import jax.numpy as jnp
from jax import lax

D = 768
FF = 3072
VOCAB = 32768
ITERS = 3
STEP = 10
NB = 9984
N_DP = 16
N_SHARD = 8


def block_levels(rng, extent, split, smallest, high):
    loudness = 1.0
    for axis_at, shards_of in split:
        draws = jax.random.uniform(jax.random.fold_in(jax.random.fold_in(rng, 6), axis_at), (shards_of,), jnp.float32, smallest / len(split), high / len(split))
        loudness = loudness * jnp.repeat(jnp.exp(draws), extent[axis_at] // shards_of).reshape((-1,) + (1,) * (len(extent) - 1 - axis_at))
    return loudness


def scatter_about(key, extent, width, bound, pieces=(), kind=jnp.bfloat16):
    level = block_levels(key, extent, pieces, -0.22, 0.18) if pieces else 1.0
    values = jax.random.normal(key, extent, jnp.float32) * width * level
    return jnp.minimum(jnp.maximum(values, -bound), bound).astype(kind)


def setup_inputs(seed: int = 0) -> dict:
    keys = jax.random.split(jax.random.key(seed), 17)
    return {
        "grad_qkv": scatter_about(keys[0], (N_DP, D, 3 * D), 0.25, 4.0, ((0, 16), (1, 8))),
        "grad_out": scatter_about(keys[1], (N_DP, D, D), 0.25, 4.0, ((0, 16), (1, 8))),
        "grad_up": scatter_about(keys[2], (N_DP, D, FF), 0.25, 4.0, ((0, 16), (1, 8))),
        "grad_down": scatter_about(keys[3], (N_DP, FF, D), 0.25, 4.0, ((0, 16), (1, 8))),
        "grad_bias": scatter_about(keys[4], (N_DP, NB), 1.0, 6.0, ((0, 16),)),
        "grad_embed": scatter_about(keys[5], (N_DP, VOCAB, D), 1.0, 6.0, ((0, 16), (1, 8))),
        "moment_qkv": scatter_about(keys[6], (D, 3 * D), 1.0, 6.0, ((0, 8),), jnp.float32),
        "moment_out": scatter_about(keys[7], (D, D), 1.0, 6.0, ((0, 8),), jnp.float32),
        "moment_up": scatter_about(keys[8], (D, FF), 1.0, 6.0, ((0, 8),), jnp.float32),
        "moment_down": scatter_about(keys[9], (FF, D), 1.0, 6.0, ((0, 8),), jnp.float32),
        "embed_param": scatter_about(keys[10], (N_SHARD, VOCAB // N_SHARD, D), 0.5, 6.0, ((0, 8), (1, 16)), jnp.float32),
        "embed_first": scatter_about(keys[11], (N_SHARD, VOCAB // N_SHARD, D), 0.5, 6.0, ((0, 8), (1, 16)), jnp.float32),
        "embed_second": jnp.clip(jnp.exp(math.log(1.0) - 4.6051702 * jax.random.uniform(keys[12], (N_SHARD, VOCAB // N_SHARD, D), jnp.float32) ** block_levels(keys[12], (N_SHARD, VOCAB // N_SHARD, D), ((0, 8), (1, 16)), -0.2, 0.2)), 0.01, 1.0),
        "bias_param": scatter_about(keys[13], (NB,), 0.5, 6.0, (), jnp.float32),
        "bias_first": scatter_about(keys[14], (NB,), 0.5, 6.0, (), jnp.float32),
        "bias_second": jnp.clip(jnp.exp(jax.random.uniform(keys[15], (NB,), jnp.float32, math.log(0.01), math.log(1.0))), 0.01, 1.0),
    }


coef_a = 3.4445
coef_b = -4.775
coef_c = 2.0315
keep_rate = 0.95
beta_one = 0.9
beta_two = 0.999
learn_rate = 0.001
decay_rate = 0.01
adam_eps = 1e-08

def orthogonalize(matrix):
    flipped = matrix.shape[0] > matrix.shape[1]
    current = matrix.T if flipped else matrix
    factor = 0.2 * max(matrix.shape) ** 0.5
    wide = current.astype(jnp.float32)
    norm_value = jnp.sqrt(jnp.sum(wide * wide))
    current = (wide / (norm_value + 1e-07)).astype(jnp.bfloat16)
    result = current
    for turn in range(ITERS):
        gram = jnp.dot(current, current.T, preferred_element_type=jnp.float32).astype(jnp.bfloat16)
        square = jnp.dot(gram, gram, preferred_element_type=jnp.float32)
        poly = (coef_b * gram.astype(jnp.float32) + coef_c * square).astype(jnp.bfloat16)
        following = coef_a * current.astype(jnp.float32) + jnp.dot(poly, current, preferred_element_type=jnp.float32)
        if turn + 1 < ITERS:
            current = following.astype(jnp.bfloat16)
        else:
            result = (factor * following).astype(jnp.bfloat16)
    return result.T if flipped else result

def muon_one(grads, moment):
    total = lax.optimization_barrier(jnp.sum(grads, axis=0, dtype=jnp.float32))
    fresh = keep_rate * moment + total
    nesterov = (total + keep_rate * fresh).astype(jnp.bfloat16)
    return (fresh, orthogonalize(nesterov))

def adamw(total, param, first, second):
    first_new = beta_one * first + (1.0 - beta_one) * total
    second_new = beta_two * second + (1.0 - beta_two) * total * total
    first_hat = first_new / (1.0 - beta_one ** STEP)
    second_hat = second_new / (1.0 - beta_two ** STEP)
    param_new = param - learn_rate * (first_hat / (jnp.sqrt(second_hat) + adam_eps) + decay_rate * param)
    return (param_new, first_new, second_new)

def reference(grad_qkv, grad_out, grad_up, grad_down, grad_bias, grad_embed, moment_qkv, moment_out, moment_up, moment_down, embed_param, embed_first, embed_second, bias_param, bias_first, bias_second):
    moment_a, update_a = muon_one(grad_qkv, moment_qkv)
    moment_b, update_b = muon_one(grad_out, moment_out)
    moment_c, update_c = muon_one(grad_up, moment_up)
    moment_d, update_d = muon_one(grad_down, moment_down)
    embed_total = lax.optimization_barrier(jnp.sum(grad_embed, axis=0, dtype=jnp.float32)).reshape(embed_param.shape)
    embed_new = adamw(embed_total, embed_param, embed_first, embed_second)
    bias_total = lax.optimization_barrier(jnp.sum(grad_bias, axis=0, dtype=jnp.float32))
    bias_new = adamw(bias_total, bias_param, bias_first, bias_second)
    return (moment_a, update_a, moment_b, update_b, moment_c, update_c, moment_d, update_d, embed_new[0], embed_new[1], embed_new[2], bias_new[0], bias_new[1], bias_new[2])
```

```python
import jax
import jax.numpy as jnp
from jax import lax
from jax.sharding import PartitionSpec as P

ITERS = 3
STEP = 10


coef_a = 3.4445
coef_b = -4.775
coef_c = 2.0315
keep_rate = 0.95
beta_one = 0.9
beta_two = 0.999
learn_rate = 0.001
decay_rate = 0.01
adam_eps = 1e-08


def newton_schulz(current, factor):
    wide = current.astype(jnp.float32)
    norm_value = jnp.sqrt(jnp.sum(wide * wide))
    current = (wide / (norm_value + 1e-07)).astype(jnp.bfloat16)
    result = current
    for turn in range(ITERS):
        gram = jnp.dot(current, current.T, preferred_element_type=jnp.float32).astype(jnp.bfloat16)
        square = jnp.dot(gram, gram, preferred_element_type=jnp.float32)
        poly = (coef_b * gram.astype(jnp.float32) + coef_c * square).astype(jnp.bfloat16)
        following = coef_a * current.astype(jnp.float32) + jnp.dot(
            poly, current, preferred_element_type=jnp.float32
        )
        if turn + 1 < ITERS:
            current = following.astype(jnp.bfloat16)
        else:
            result = (factor * following).astype(jnp.bfloat16)
    return result


def adamw(total, param, first, second):
    first_new = beta_one * first + (1.0 - beta_one) * total
    second_new = beta_two * second + (1.0 - beta_two) * total * total
    first_hat = first_new / (1.0 - beta_one**STEP)
    second_hat = second_new / (1.0 - beta_two**STEP)
    param_new = param - learn_rate * (
        first_hat / (jnp.sqrt(second_hat) + adam_eps) + decay_rate * param
    )
    return (param_new, first_new, second_new)


def local(
    grad_qkv,
    grad_out,
    grad_up,
    grad_down,
    grad_bias,
    grad_embed,
    moment_qkv,
    moment_out,
    moment_up,
    moment_down,
    embed_param,
    embed_first,
    embed_second,
    bias_param,
    bias_first,
    bias_second,
):
    groups = lax.axis_size("shard")
    myself = lax.axis_index("shard")
    grads = (grad_qkv[0], grad_out[0], grad_up[0], grad_down[0], grad_bias[0])
    sums = lax.psum(grads, "dp")
    moments_old = (moment_qkv, moment_out, moment_up, moment_down)
    new_moments = []
    nesterov = []
    for which in range(4):
        total = sums[which].astype(jnp.float32)
        fresh = keep_rate * moments_old[which] + total
        new_moments.append(fresh)
        nesterov.append((total + keep_rate * fresh).astype(jnp.bfloat16))

    shapes = [(p.shape[0] * groups, p.shape[1]) for p in nesterov]
    wide_rows = max(min(s) for s in shapes)
    wide_cols = max(max(s) for s in shapes)
    slot = max(p.size for p in nesterov)
    owners = [which * groups // 4 for which in range(4)]
    owned = jnp.int32(4)
    for which in range(4):
        owned = jnp.where(myself == owners[which], which, owned)

    pieces = [jnp.zeros((slot,), jnp.bfloat16)] * groups
    for which in range(4):
        flat = nesterov[which].reshape(-1)
        pieces[owners[which]] = jnp.pad(flat, (0, slot - flat.shape[0]))
    outgoing = jnp.stack(pieces)
    incoming = lax.all_to_all(outgoing, "shard", 0, 0, tiled=True)

    def assemble(which):
        rows, cols = shapes[which]

        def branch(buffer):
            whole = buffer[:, : (rows // groups) * cols].reshape(rows, cols)
            if rows > cols:
                whole = whole.T
            r, c = whole.shape
            return jnp.pad(whole, ((0, wide_rows - r), (0, wide_cols - c)))

        return branch

    def nothing(buffer):
        return jnp.zeros((wide_rows, wide_cols), jnp.bfloat16)

    matrix = lax.switch(owned, [assemble(w) for w in range(4)] + [nothing], incoming)
    factors = jnp.array([0.2 * max(s) ** 0.5 for s in shapes] + [0.0], jnp.float32)
    result = newton_schulz(matrix, factors[owned])

    def disassemble(which):
        rows, cols = shapes[which]

        def branch(y):
            if rows > cols:
                part = y[:cols, :rows].T
            else:
                part = y[:rows, :cols]
            flat = part.reshape(groups, (rows // groups) * cols)
            return jnp.pad(flat, ((0, 0), (0, slot - flat.shape[1])))

        return branch

    def nothing_back(y):
        return jnp.zeros((groups, slot), jnp.bfloat16)

    answered = lax.switch(owned, [disassemble(w) for w in range(4)] + [nothing_back], result)
    returned = lax.all_to_all(answered, "shard", 0, 0, tiled=True)
    updates = [
        returned[owners[which], : nesterov[which].size].reshape(nesterov[which].shape)
        for which in range(4)
    ]

    _, grad_embed = lax.optimization_barrier((sums, grad_embed))
    embed_total = lax.psum_scatter(grad_embed, "dp", scatter_dimension=1, tiled=True).astype(
        jnp.float32
    )
    embed_new = adamw(embed_total, embed_param, embed_first, embed_second)
    bias_new = adamw(sums[4].astype(jnp.float32), bias_param, bias_first, bias_second)
    return (
        new_moments[0],
        updates[0],
        new_moments[1],
        updates[1],
        new_moments[2],
        updates[2],
        new_moments[3],
        updates[3],
        embed_new[0],
        embed_new[1],
        embed_new[2],
        bias_new[0],
        bias_new[1],
        bias_new[2],
    )


def solution(mesh):
    placed = (
        P("dp", "shard", None),
        P("dp", "shard", None),
        P("dp", "shard", None),
        P("dp", "shard", None),
        P("dp", None),
        P("dp", "shard", None),
        P("shard", None),
        P("shard", None),
        P("shard", None),
        P("shard", None),
        P("shard", "dp", None),
        P("shard", "dp", None),
        P("shard", "dp", None),
        P(),
        P(),
        P(),
    )
    return jax.shard_map(
        local,
        mesh=mesh,
        in_specs=placed,
        out_specs=(
            P("shard", None),
            P("shard", None),
            P("shard", None),
            P("shard", None),
            P("shard", None),
            P("shard", None),
            P("shard", None),
            P("shard", None),
            P("shard", "dp", None),
            P("shard", "dp", None),
            P("shard", "dp", None),
            P(),
            P(),
            P(),
        ),
        check_vma=False,
    )
```

```python
import jax
import jax.numpy as jnp
from jax import lax
from jax.sharding import PartitionSpec as P

ITERS = 3
STEP = 10


coef_a = 3.4445
coef_b = -4.775
coef_c = 2.0315
keep_rate = 0.95
beta_one = 0.9
beta_two = 0.999
learn_rate = 0.001
decay_rate = 0.01
adam_eps = 1e-08


def newton_schulz(current, factor):
    wide = current.astype(jnp.float32)
    norm_value = jnp.sqrt(jnp.sum(wide * wide))
    current = (wide / (norm_value + 1e-07)).astype(jnp.bfloat16)
    result = current
    for turn in range(ITERS):
        gram = jnp.dot(current, current.T, preferred_element_type=jnp.float32).astype(jnp.bfloat16)
        square = jnp.dot(gram, gram, preferred_element_type=jnp.float32)
        poly = (coef_b * gram.astype(jnp.float32) + coef_c * square).astype(jnp.bfloat16)
        following = coef_a * current.astype(jnp.float32) + jnp.dot(
            poly, current, preferred_element_type=jnp.float32
        )
        if turn + 1 < ITERS:
            current = following.astype(jnp.bfloat16)
        else:
            result = (factor * following).astype(jnp.bfloat16)
    return result


def adamw(total, param, first, second):
    first_new = beta_one * first + (1.0 - beta_one) * total
    second_new = beta_two * second + (1.0 - beta_two) * total * total
    first_hat = first_new / (1.0 - beta_one**STEP)
    second_hat = second_new / (1.0 - beta_two**STEP)
    param_new = param - learn_rate * (
        first_hat / (jnp.sqrt(second_hat) + adam_eps) + decay_rate * param
    )
    return (param_new, first_new, second_new)


def local(
    grad_qkv,
    grad_out,
    grad_up,
    grad_down,
    grad_bias,
    grad_embed,
    moment_qkv,
    moment_out,
    moment_up,
    moment_down,
    embed_param,
    embed_first,
    embed_second,
    bias_param,
    bias_first,
    bias_second,
):
    groups = lax.axis_size("shard")
    replicas = lax.axis_size("dp")
    myself = lax.axis_index("shard")
    lanes = 128
    grads = (grad_qkv[0], grad_out[0], grad_up[0], grad_down[0], grad_bias[0])
    sizes = [g.size for g in grads]
    flat = jnp.concatenate([g.reshape(-1) for g in grads])
    block = replicas * 16 * lanes
    padded = -(-flat.shape[0] // block) * block
    flat = jnp.pad(flat, (0, padded - flat.shape[0])).reshape(padded // lanes, lanes)
    reduced = lax.psum_scatter(flat, "dp", scatter_dimension=0, tiled=True)
    gathered = lax.all_gather(reduced, "dp", axis=0, tiled=True).reshape(-1)
    sums = []
    offset = 0
    for g, n in zip(grads, sizes):
        sums.append(gathered[offset : offset + n].reshape(g.shape))
        offset += n
    moments_old = (moment_qkv, moment_out, moment_up, moment_down)
    new_moments = []
    nesterov = []
    for which in range(4):
        total = sums[which].astype(jnp.float32)
        fresh = keep_rate * moments_old[which] + total
        new_moments.append(fresh)
        nesterov.append((total + keep_rate * fresh).astype(jnp.bfloat16))

    shapes = [(p.shape[0] * groups, p.shape[1]) for p in nesterov]
    wide_rows = max(min(s) for s in shapes)
    wide_cols = max(max(s) for s in shapes)
    slot = max(p.size for p in nesterov) // lanes
    owners = [which * groups // 4 for which in range(4)]
    owned = jnp.int32(4)
    for which in range(4):
        owned = jnp.where(myself == owners[which], which, owned)

    pieces = [jnp.zeros((slot, lanes), jnp.bfloat16)] * groups
    for which in range(4):
        part = nesterov[which].reshape(-1, lanes)
        pieces[owners[which]] = jnp.pad(part, ((0, slot - part.shape[0]), (0, 0)))
    outgoing = jnp.stack(pieces)
    incoming = lax.all_to_all(outgoing, "shard", 0, 0, tiled=True)

    def assemble(which):
        rows, cols = shapes[which]

        def branch(buffer):
            used = (rows // groups) * cols // lanes
            whole = buffer[:, :used, :].reshape(rows, cols)
            if rows > cols:
                whole = whole.T
            r, c = whole.shape
            return jnp.pad(whole, ((0, wide_rows - r), (0, wide_cols - c)))

        return branch

    def nothing(buffer):
        return jnp.zeros((wide_rows, wide_cols), jnp.bfloat16)

    matrix = lax.switch(owned, [assemble(w) for w in range(4)] + [nothing], incoming)
    factors = jnp.array([0.2 * max(s) ** 0.5 for s in shapes] + [0.0], jnp.float32)
    result = newton_schulz(matrix, factors[owned])

    def disassemble(which):
        rows, cols = shapes[which]

        def branch(y):
            if rows > cols:
                part = y[:cols, :rows].T
            else:
                part = y[:rows, :cols]
            part = part.reshape(groups, -1, lanes)
            return jnp.pad(part, ((0, 0), (0, slot - part.shape[1]), (0, 0)))

        return branch

    def nothing_back(y):
        return jnp.zeros((groups, slot, lanes), jnp.bfloat16)

    answered = lax.switch(owned, [disassemble(w) for w in range(4)] + [nothing_back], result)
    returned = lax.all_to_all(answered, "shard", 0, 0, tiled=True)
    updates = [
        returned[owners[which], : nesterov[which].size // lanes, :].reshape(nesterov[which].shape)
        for which in range(4)
    ]

    _, grad_embed = lax.optimization_barrier((gathered, grad_embed))
    embed_total = lax.psum_scatter(grad_embed, "dp", scatter_dimension=1, tiled=True).astype(
        jnp.float32
    )
    embed_new = adamw(embed_total, embed_param, embed_first, embed_second)
    bias_new = adamw(sums[4].astype(jnp.float32), bias_param, bias_first, bias_second)
    return (
        new_moments[0],
        updates[0],
        new_moments[1],
        updates[1],
        new_moments[2],
        updates[2],
        new_moments[3],
        updates[3],
        embed_new[0],
        embed_new[1],
        embed_new[2],
        bias_new[0],
        bias_new[1],
        bias_new[2],
    )


def solution(mesh):
    placed = (
        P("dp", "shard", None),
        P("dp", "shard", None),
        P("dp", "shard", None),
        P("dp", "shard", None),
        P("dp", None),
        P("dp", "shard", None),
        P("shard", None),
        P("shard", None),
        P("shard", None),
        P("shard", None),
        P("shard", "dp", None),
        P("shard", "dp", None),
        P("shard", "dp", None),
        P(),
        P(),
        P(),
    )
    return jax.shard_map(
        local,
        mesh=mesh,
        in_specs=placed,
        out_specs=(
            P("shard", None),
            P("shard", None),
            P("shard", None),
            P("shard", None),
            P("shard", None),
            P("shard", None),
            P("shard", None),
            P("shard", None),
            P("shard", "dp", None),
            P("shard", "dp", None),
            P("shard", "dp", None),
            P(),
            P(),
            P(),
        ),
        check_vma=False,
    )
```

```python
import jax
import jax.numpy as jnp
from jax import lax
from jax.sharding import PartitionSpec as P

ITERS = 3
STEP = 10


coef_a = 3.4445
coef_b = -4.775
coef_c = 2.0315
keep_rate = 0.95
beta_one = 0.9
beta_two = 0.999
learn_rate = 0.001
decay_rate = 0.01
adam_eps = 1e-08


def newton_schulz(current, factor):
    wide = current.astype(jnp.float32)
    norm_value = jnp.sqrt(jnp.sum(wide * wide))
    current = (wide / (norm_value + 1e-07)).astype(jnp.bfloat16)
    result = current
    for turn in range(ITERS):
        gram = jnp.dot(current, current.T, preferred_element_type=jnp.float32).astype(jnp.bfloat16)
        square = jnp.dot(gram, gram, preferred_element_type=jnp.float32)
        poly = (coef_b * gram.astype(jnp.float32) + coef_c * square).astype(jnp.bfloat16)
        following = coef_a * current.astype(jnp.float32) + jnp.dot(
            poly, current, preferred_element_type=jnp.float32
        )
        if turn + 1 < ITERS:
            current = following.astype(jnp.bfloat16)
        else:
            result = (factor * following).astype(jnp.bfloat16)
    return result


def adamw(total, param, first, second):
    first_new = beta_one * first + (1.0 - beta_one) * total
    second_new = beta_two * second + (1.0 - beta_two) * total * total
    first_hat = first_new / (1.0 - beta_one**STEP)
    second_hat = second_new / (1.0 - beta_two**STEP)
    param_new = param - learn_rate * (
        first_hat / (jnp.sqrt(second_hat) + adam_eps) + decay_rate * param
    )
    return (param_new, first_new, second_new)


def local(
    grad_qkv,
    grad_out,
    grad_up,
    grad_down,
    grad_bias,
    grad_embed,
    moment_qkv,
    moment_out,
    moment_up,
    moment_down,
    embed_param,
    embed_first,
    embed_second,
    bias_param,
    bias_first,
    bias_second,
):
    groups = lax.axis_size("shard")
    replicas = lax.axis_size("dp")
    myself = lax.axis_index("shard")
    lanes = 128
    grads = (grad_qkv[0], grad_out[0], grad_up[0], grad_down[0], grad_bias[0])
    sizes = [g.size for g in grads]
    flat = jnp.concatenate([g.reshape(-1) for g in grads])
    block = replicas * 16 * lanes
    padded = -(-flat.shape[0] // block) * block
    flat = jnp.pad(flat, (0, padded - flat.shape[0])).reshape(padded // lanes, lanes)
    reduced = lax.psum_scatter(flat, "dp", scatter_dimension=0, tiled=True)
    gathered = lax.all_gather(reduced, "dp", axis=0, tiled=True).reshape(-1)
    sums = []
    offset = 0
    for g, n in zip(grads, sizes):
        sums.append(gathered[offset : offset + n].reshape(g.shape))
        offset += n
    moments_old = (moment_qkv, moment_out, moment_up, moment_down)
    new_moments = []
    nesterov = []
    for which in range(4):
        total = sums[which].astype(jnp.float32)
        fresh = keep_rate * moments_old[which] + total
        new_moments.append(fresh)
        nesterov.append((total + keep_rate * fresh).astype(jnp.bfloat16))

    shapes = [(p.shape[0] * groups, p.shape[1]) for p in nesterov]
    wide_rows = max(min(s) for s in shapes)
    wide_cols = max(max(s) for s in shapes)
    slot = max(p.size for p in nesterov) // lanes
    owners = [which * groups // 4 for which in range(4)]
    owned = jnp.int32(4)
    for which in range(4):
        owned = jnp.where(myself == owners[which], which, owned)

    pieces = [jnp.zeros((slot, lanes), jnp.bfloat16)] * groups
    for which in range(4):
        part = nesterov[which].reshape(-1, lanes)
        pieces[owners[which]] = jnp.pad(part, ((0, slot - part.shape[0]), (0, 0)))
    outgoing = jnp.stack(pieces)
    incoming = lax.all_to_all(outgoing, "shard", 0, 0, tiled=True)

    def assemble(which):
        rows, cols = shapes[which]

        def branch(buffer):
            used = (rows // groups) * cols // lanes
            whole = buffer[:, :used, :].reshape(rows, cols)
            if rows > cols:
                whole = whole.T
            r, c = whole.shape
            return jnp.pad(whole, ((0, wide_rows - r), (0, wide_cols - c)))

        return branch

    def nothing(buffer):
        return jnp.zeros((wide_rows, wide_cols), jnp.bfloat16)

    matrix = lax.switch(owned, [assemble(w) for w in range(4)] + [nothing], incoming)
    factors = jnp.array([0.2 * max(s) ** 0.5 for s in shapes] + [0.0], jnp.float32)
    result = newton_schulz(matrix, factors[owned])

    def disassemble(which):
        rows, cols = shapes[which]

        def branch(y):
            if rows > cols:
                part = y[:cols, :rows].T
            else:
                part = y[:rows, :cols]
            part = part.reshape(groups, -1, lanes)
            return jnp.pad(part, ((0, 0), (0, slot - part.shape[1]), (0, 0)))

        return branch

    def nothing_back(y):
        return jnp.zeros((groups, slot, lanes), jnp.bfloat16)

    answered = lax.switch(owned, [disassemble(w) for w in range(4)] + [nothing_back], result)
    returned = lax.all_to_all(answered, "shard", 0, 0, tiled=True)
    updates = [
        returned[owners[which], : nesterov[which].size // lanes, :].reshape(nesterov[which].shape)
        for which in range(4)
    ]

    _, grad_embed = lax.optimization_barrier((incoming, grad_embed))
    embed_total = lax.psum_scatter(grad_embed, "dp", scatter_dimension=1, tiled=True).astype(
        jnp.float32
    )
    embed_new = adamw(embed_total, embed_param, embed_first, embed_second)
    bias_new = adamw(sums[4].astype(jnp.float32), bias_param, bias_first, bias_second)
    return (
        new_moments[0],
        updates[0],
        new_moments[1],
        updates[1],
        new_moments[2],
        updates[2],
        new_moments[3],
        updates[3],
        embed_new[0],
        embed_new[1],
        embed_new[2],
        bias_new[0],
        bias_new[1],
        bias_new[2],
    )


def solution(mesh):
    placed = (
        P("dp", "shard", None),
        P("dp", "shard", None),
        P("dp", "shard", None),
        P("dp", "shard", None),
        P("dp", None),
        P("dp", "shard", None),
        P("shard", None),
        P("shard", None),
        P("shard", None),
        P("shard", None),
        P("shard", "dp", None),
        P("shard", "dp", None),
        P("shard", "dp", None),
        P(),
        P(),
        P(),
    )
    return jax.shard_map(
        local,
        mesh=mesh,
        in_specs=placed,
        out_specs=(
            P("shard", None),
            P("shard", None),
            P("shard", None),
            P("shard", None),
            P("shard", None),
            P("shard", None),
            P("shard", None),
            P("shard", None),
            P("shard", "dp", None),
            P("shard", "dp", None),
            P("shard", "dp", None),
            P(),
            P(),
            P(),
        ),
        check_vma=False,
    )
```

```python
import jax
import jax.numpy as jnp
from jax import lax
from jax.sharding import PartitionSpec as P

ITERS = 3
STEP = 10


coef_a = 3.4445
coef_b = -4.775
coef_c = 2.0315
keep_rate = 0.95
beta_one = 0.9
beta_two = 0.999
learn_rate = 0.001
decay_rate = 0.01
adam_eps = 1e-08


def newton_schulz(current, factor, exchange):
    wide = current.astype(jnp.float32)
    squares = jnp.sum(wide * wide)
    norm_value = jnp.sqrt(squares + exchange(squares))
    current = (wide / (norm_value + 1e-07)).astype(jnp.bfloat16)
    result = current
    for turn in range(ITERS):
        part = jnp.dot(current, current.T, preferred_element_type=jnp.float32)
        gram = (part + exchange(part)).astype(jnp.bfloat16)
        square = jnp.dot(gram, gram, preferred_element_type=jnp.float32)
        poly = (coef_b * gram.astype(jnp.float32) + coef_c * square).astype(jnp.bfloat16)
        following = coef_a * current.astype(jnp.float32) + jnp.dot(
            poly, current, preferred_element_type=jnp.float32
        )
        if turn + 1 < ITERS:
            current = following.astype(jnp.bfloat16)
        else:
            result = (factor * following).astype(jnp.bfloat16)
    return result


def adamw(total, param, first, second):
    first_new = beta_one * first + (1.0 - beta_one) * total
    second_new = beta_two * second + (1.0 - beta_two) * total * total
    first_hat = first_new / (1.0 - beta_one**STEP)
    second_hat = second_new / (1.0 - beta_two**STEP)
    param_new = param - learn_rate * (
        first_hat / (jnp.sqrt(second_hat) + adam_eps) + decay_rate * param
    )
    return (param_new, first_new, second_new)


def local(
    grad_qkv,
    grad_out,
    grad_up,
    grad_down,
    grad_bias,
    grad_embed,
    moment_qkv,
    moment_out,
    moment_up,
    moment_down,
    embed_param,
    embed_first,
    embed_second,
    bias_param,
    bias_first,
    bias_second,
):
    groups = lax.axis_size("shard")
    replicas = lax.axis_size("dp")
    myself = lax.axis_index("shard")
    lanes = 128
    grads = (grad_qkv[0], grad_out[0], grad_up[0], grad_down[0], grad_bias[0])
    sizes = [g.size for g in grads]
    flat = jnp.concatenate([g.reshape(-1) for g in grads])
    block = replicas * 16 * lanes
    padded = -(-flat.shape[0] // block) * block
    flat = jnp.pad(flat, (0, padded - flat.shape[0])).reshape(padded // lanes, lanes)
    reduced = lax.psum_scatter(flat, "dp", scatter_dimension=0, tiled=True)
    gathered = lax.all_gather(reduced, "dp", axis=0, tiled=True).reshape(-1)
    sums = []
    offset = 0
    for g, n in zip(grads, sizes):
        sums.append(gathered[offset : offset + n].reshape(g.shape))
        offset += n
    moments_old = (moment_qkv, moment_out, moment_up, moment_down)
    new_moments = []
    nesterov = []
    for which in range(4):
        total = sums[which].astype(jnp.float32)
        fresh = keep_rate * moments_old[which] + total
        new_moments.append(fresh)
        nesterov.append((total + keep_rate * fresh).astype(jnp.bfloat16))

    core = lax.axis_index("dp") % 2
    partner = [(d, d ^ 1) for d in range(replicas)]

    def exchange(value):
        return lax.ppermute(value, "dp", partner)

    shapes = [(p.shape[0] * groups, p.shape[1]) for p in nesterov]
    flipped = [rows > cols for rows, cols in shapes]
    wide_rows = max(min(s) for s in shapes)
    half_cols = max(max(s) for s in shapes) // 2
    halves = []
    for which in range(4):
        part = nesterov[which]
        axis = 0 if flipped[which] else 1
        size = part.shape[axis] // 2
        halves.append(lax.dynamic_slice_in_dim(part, core * size, size, axis))
    slot = max(h.size for h in halves) // lanes
    owners = [which * groups // 4 for which in range(4)]
    owned = jnp.int32(4)
    for which in range(4):
        owned = jnp.where(myself == owners[which], which, owned)

    pieces = [jnp.zeros((slot, lanes), jnp.bfloat16)] * groups
    for which in range(4):
        part = halves[which].reshape(-1, lanes)
        pieces[owners[which]] = jnp.pad(part, ((0, slot - part.shape[0]), (0, 0)))
    outgoing = jnp.stack(pieces)
    incoming = lax.all_to_all(outgoing, "shard", 0, 0, tiled=True)

    def assemble(which):
        hr, hc = halves[which].shape

        def branch(buffer):
            used = hr * hc // lanes
            whole = buffer[:, :used, :].reshape(groups * hr, hc)
            if flipped[which]:
                whole = whole.T
            r, c = whole.shape
            return jnp.pad(whole, ((0, wide_rows - r), (0, half_cols - c)))

        return branch

    def nothing(buffer):
        return jnp.zeros((wide_rows, half_cols), jnp.bfloat16)

    matrix = lax.switch(owned, [assemble(w) for w in range(4)] + [nothing], incoming)
    factors = jnp.array([0.2 * max(s) ** 0.5 for s in shapes] + [0.0], jnp.float32)
    result = newton_schulz(matrix, factors[owned], exchange)

    def disassemble(which):
        hr, hc = halves[which].shape

        def branch(y):
            if flipped[which]:
                part = y[:hc, : groups * hr].T
            else:
                part = y[: groups * hr, :hc]
            part = part.reshape(groups, -1, lanes)
            return jnp.pad(part, ((0, 0), (0, slot - part.shape[1]), (0, 0)))

        return branch

    def nothing_back(y):
        return jnp.zeros((groups, slot, lanes), jnp.bfloat16)

    answered = lax.switch(owned, [disassemble(w) for w in range(4)] + [nothing_back], result)
    returned = lax.all_to_all(answered, "shard", 0, 0, tiled=True)
    mine = jnp.stack([returned[owners[which]] for which in range(4)])
    theirs = exchange(mine)
    first = core == 0
    updates = []
    for which in range(4):
        hr, hc = halves[which].shape
        used = hr * hc // lanes
        own = mine[which, :used].reshape(hr, hc)
        other = theirs[which, :used].reshape(hr, hc)
        low = jnp.where(first, own, other)
        high = jnp.where(first, other, own)
        updates.append(jnp.concatenate([low, high], axis=0 if flipped[which] else 1))

    _, grad_embed = lax.optimization_barrier((incoming, grad_embed))
    embed_total = lax.psum_scatter(grad_embed, "dp", scatter_dimension=1, tiled=True).astype(
        jnp.float32
    )
    embed_new = adamw(embed_total, embed_param, embed_first, embed_second)
    bias_new = adamw(sums[4].astype(jnp.float32), bias_param, bias_first, bias_second)
    return (
        new_moments[0],
        updates[0],
        new_moments[1],
        updates[1],
        new_moments[2],
        updates[2],
        new_moments[3],
        updates[3],
        embed_new[0],
        embed_new[1],
        embed_new[2],
        bias_new[0],
        bias_new[1],
        bias_new[2],
    )


def solution(mesh):
    placed = (
        P("dp", "shard", None),
        P("dp", "shard", None),
        P("dp", "shard", None),
        P("dp", "shard", None),
        P("dp", None),
        P("dp", "shard", None),
        P("shard", None),
        P("shard", None),
        P("shard", None),
        P("shard", None),
        P("shard", "dp", None),
        P("shard", "dp", None),
        P("shard", "dp", None),
        P(),
        P(),
        P(),
    )
    return jax.shard_map(
        local,
        mesh=mesh,
        in_specs=placed,
        out_specs=(
            P("shard", None),
            P("shard", None),
            P("shard", None),
            P("shard", None),
            P("shard", None),
            P("shard", None),
            P("shard", None),
            P("shard", None),
            P("shard", "dp", None),
            P("shard", "dp", None),
            P("shard", "dp", None),
            P(),
            P(),
            P(),
        ),
        check_vma=False,
    )
```

```python
import jax
import jax.numpy as jnp
from jax import lax
from jax.sharding import PartitionSpec as P

ITERS = 3
STEP = 10


coef_a = 3.4445
coef_b = -4.775
coef_c = 2.0315
keep_rate = 0.95
beta_one = 0.9
beta_two = 0.999
learn_rate = 0.001
decay_rate = 0.01
adam_eps = 1e-08


def newton_schulz(current, factor, exchange):
    wide = current.astype(jnp.float32)
    squares = jnp.sum(wide * wide)
    norm_value = jnp.sqrt(squares + exchange(squares))
    current = (wide / (norm_value + 1e-07)).astype(jnp.bfloat16)
    result = current
    for turn in range(ITERS):
        part = jnp.dot(current, current.T, preferred_element_type=jnp.float32)
        gram = (part + exchange(part)).astype(jnp.bfloat16)
        square = jnp.dot(gram, gram, preferred_element_type=jnp.float32)
        poly = (coef_b * gram.astype(jnp.float32) + coef_c * square).astype(jnp.bfloat16)
        following = coef_a * current.astype(jnp.float32) + jnp.dot(
            poly, current, preferred_element_type=jnp.float32
        )
        if turn + 1 < ITERS:
            current = following.astype(jnp.bfloat16)
        else:
            result = (factor * following).astype(jnp.bfloat16)
    return result


def adamw(total, param, first, second):
    first_new = beta_one * first + (1.0 - beta_one) * total
    second_new = beta_two * second + (1.0 - beta_two) * total * total
    first_hat = first_new / (1.0 - beta_one**STEP)
    second_hat = second_new / (1.0 - beta_two**STEP)
    param_new = param - learn_rate * (
        first_hat / (jnp.sqrt(second_hat) + adam_eps) + decay_rate * param
    )
    return (param_new, first_new, second_new)


def local(
    grad_qkv,
    grad_out,
    grad_up,
    grad_down,
    grad_bias,
    grad_embed,
    moment_qkv,
    moment_out,
    moment_up,
    moment_down,
    embed_param,
    embed_first,
    embed_second,
    bias_param,
    bias_first,
    bias_second,
):
    groups = lax.axis_size("shard")
    replicas = lax.axis_size("dp")
    myself = lax.axis_index("shard")
    lanes = 128
    grads = (grad_qkv[0], grad_out[0], grad_up[0], grad_down[0], grad_bias[0])
    sizes = [g.size for g in grads]
    flat = jnp.concatenate([g.reshape(-1) for g in grads])
    block = replicas * 16 * lanes
    padded = -(-flat.shape[0] // block) * block
    flat = jnp.pad(flat, (0, padded - flat.shape[0])).reshape(padded // lanes, lanes)
    parts = lax.all_to_all(flat.reshape(replicas, -1, lanes), "dp", 0, 0, tiled=True)
    reduced = jnp.sum(parts.astype(jnp.float32), axis=0).astype(jnp.bfloat16)
    gathered = lax.all_gather(reduced, "dp", axis=0, tiled=True).reshape(-1)
    sums = []
    offset = 0
    for g, n in zip(grads, sizes):
        sums.append(gathered[offset : offset + n].reshape(g.shape))
        offset += n
    moments_old = (moment_qkv, moment_out, moment_up, moment_down)
    new_moments = []
    nesterov = []
    for which in range(4):
        total = sums[which].astype(jnp.float32)
        fresh = keep_rate * moments_old[which] + total
        new_moments.append(fresh)
        nesterov.append((total + keep_rate * fresh).astype(jnp.bfloat16))

    core = lax.axis_index("dp") % 2
    partner = [(d, d ^ 1) for d in range(replicas)]

    def exchange(value):
        return lax.ppermute(value, "dp", partner)

    shapes = [(p.shape[0] * groups, p.shape[1]) for p in nesterov]
    flipped = [rows > cols for rows, cols in shapes]
    wide_rows = max(min(s) for s in shapes)
    half_cols = max(max(s) for s in shapes) // 2
    halves = []
    for which in range(4):
        part = nesterov[which]
        axis = 0 if flipped[which] else 1
        size = part.shape[axis] // 2
        halves.append(lax.dynamic_slice_in_dim(part, core * size, size, axis))
    slot = max(h.size for h in halves) // lanes
    owners = [which * groups // 4 for which in range(4)]
    owned = jnp.int32(4)
    for which in range(4):
        owned = jnp.where(myself == owners[which], which, owned)

    pieces = [jnp.zeros((slot, lanes), jnp.bfloat16)] * groups
    for which in range(4):
        part = halves[which].reshape(-1, lanes)
        pieces[owners[which]] = jnp.pad(part, ((0, slot - part.shape[0]), (0, 0)))
    outgoing = jnp.stack(pieces)
    incoming = lax.all_to_all(outgoing, "shard", 0, 0, tiled=True)

    def assemble(which):
        hr, hc = halves[which].shape

        def branch(buffer):
            used = hr * hc // lanes
            whole = buffer[:, :used, :].reshape(groups * hr, hc)
            if flipped[which]:
                whole = whole.T
            r, c = whole.shape
            return jnp.pad(whole, ((0, wide_rows - r), (0, half_cols - c)))

        return branch

    def nothing(buffer):
        return jnp.zeros((wide_rows, half_cols), jnp.bfloat16)

    matrix = lax.switch(owned, [assemble(w) for w in range(4)] + [nothing], incoming)
    factors = jnp.array([0.2 * max(s) ** 0.5 for s in shapes] + [0.0], jnp.float32)
    result = newton_schulz(matrix, factors[owned], exchange)

    def disassemble(which):
        hr, hc = halves[which].shape

        def branch(y):
            if flipped[which]:
                part = y[:hc, : groups * hr].T
            else:
                part = y[: groups * hr, :hc]
            part = part.reshape(groups, -1, lanes)
            return jnp.pad(part, ((0, 0), (0, slot - part.shape[1]), (0, 0)))

        return branch

    def nothing_back(y):
        return jnp.zeros((groups, slot, lanes), jnp.bfloat16)

    answered = lax.switch(owned, [disassemble(w) for w in range(4)] + [nothing_back], result)
    returned = lax.all_to_all(answered, "shard", 0, 0, tiled=True)
    mine = jnp.stack([returned[owners[which]] for which in range(4)])
    theirs = exchange(mine)
    first = core == 0
    updates = []
    for which in range(4):
        hr, hc = halves[which].shape
        used = hr * hc // lanes
        own = mine[which, :used].reshape(hr, hc)
        other = theirs[which, :used].reshape(hr, hc)
        low = jnp.where(first, own, other)
        high = jnp.where(first, other, own)
        updates.append(jnp.concatenate([low, high], axis=0 if flipped[which] else 1))

    _, grad_embed = lax.optimization_barrier((incoming, grad_embed))
    embed_total = lax.psum_scatter(grad_embed, "dp", scatter_dimension=1, tiled=True).astype(
        jnp.float32
    )
    embed_new = adamw(embed_total, embed_param, embed_first, embed_second)
    bias_new = adamw(sums[4].astype(jnp.float32), bias_param, bias_first, bias_second)
    return (
        new_moments[0],
        updates[0],
        new_moments[1],
        updates[1],
        new_moments[2],
        updates[2],
        new_moments[3],
        updates[3],
        embed_new[0],
        embed_new[1],
        embed_new[2],
        bias_new[0],
        bias_new[1],
        bias_new[2],
    )


def solution(mesh):
    placed = (
        P("dp", "shard", None),
        P("dp", "shard", None),
        P("dp", "shard", None),
        P("dp", "shard", None),
        P("dp", None),
        P("dp", "shard", None),
        P("shard", None),
        P("shard", None),
        P("shard", None),
        P("shard", None),
        P("shard", "dp", None),
        P("shard", "dp", None),
        P("shard", "dp", None),
        P(),
        P(),
        P(),
    )
    return jax.shard_map(
        local,
        mesh=mesh,
        in_specs=placed,
        out_specs=(
            P("shard", None),
            P("shard", None),
            P("shard", None),
            P("shard", None),
            P("shard", None),
            P("shard", None),
            P("shard", None),
            P("shard", None),
            P("shard", "dp", None),
            P("shard", "dp", None),
            P("shard", "dp", None),
            P(),
            P(),
            P(),
        ),
        check_vma=False,
    )
```

```python
import jax
import jax.numpy as jnp
from jax import lax
from jax.sharding import PartitionSpec as P

ITERS = 3
STEP = 10


coef_a = 3.4445
coef_b = -4.775
coef_c = 2.0315
keep_rate = 0.95
beta_one = 0.9
beta_two = 0.999
learn_rate = 0.001
decay_rate = 0.01
adam_eps = 1e-08


def newton_schulz(current, factor, exchange):
    wide = current.astype(jnp.float32)
    squares = jnp.sum(wide * wide)
    norm_value = jnp.sqrt(squares + exchange(squares))
    current = (wide / (norm_value + 1e-07)).astype(jnp.bfloat16)
    result = current
    for turn in range(ITERS):
        part = jnp.dot(current, current.T, preferred_element_type=jnp.bfloat16)
        gram = (part.astype(jnp.float32) + exchange(part).astype(jnp.float32)).astype(jnp.bfloat16)
        square = jnp.dot(gram, gram, preferred_element_type=jnp.float32)
        poly = (coef_b * gram.astype(jnp.float32) + coef_c * square).astype(jnp.bfloat16)
        following = coef_a * current.astype(jnp.float32) + jnp.dot(
            poly, current, preferred_element_type=jnp.float32
        )
        if turn + 1 < ITERS:
            current = following.astype(jnp.bfloat16)
        else:
            result = (factor * following).astype(jnp.bfloat16)
    return result


def adamw(total, param, first, second):
    first_new = beta_one * first + (1.0 - beta_one) * total
    second_new = beta_two * second + (1.0 - beta_two) * total * total
    first_hat = first_new / (1.0 - beta_one**STEP)
    second_hat = second_new / (1.0 - beta_two**STEP)
    param_new = param - learn_rate * (
        first_hat / (jnp.sqrt(second_hat) + adam_eps) + decay_rate * param
    )
    return (param_new, first_new, second_new)


def local(
    grad_qkv,
    grad_out,
    grad_up,
    grad_down,
    grad_bias,
    grad_embed,
    moment_qkv,
    moment_out,
    moment_up,
    moment_down,
    embed_param,
    embed_first,
    embed_second,
    bias_param,
    bias_first,
    bias_second,
):
    groups = lax.axis_size("shard")
    replicas = lax.axis_size("dp")
    myself = lax.axis_index("shard")
    lanes = 128
    grads = (grad_qkv[0], grad_out[0], grad_up[0], grad_down[0], grad_bias[0])
    sizes = [g.size for g in grads]
    flat = jnp.concatenate([g.reshape(-1) for g in grads])
    block = replicas * 16 * lanes
    padded = -(-flat.shape[0] // block) * block
    flat = jnp.pad(flat, (0, padded - flat.shape[0])).reshape(padded // lanes, lanes)
    parts = lax.all_to_all(flat.reshape(replicas, -1, lanes), "dp", 0, 0, tiled=True)
    reduced = jnp.sum(parts.astype(jnp.float32), axis=0).astype(jnp.bfloat16)
    gathered = lax.all_gather(reduced, "dp", axis=0, tiled=True).reshape(-1)
    sums = []
    offset = 0
    for g, n in zip(grads, sizes):
        sums.append(gathered[offset : offset + n].reshape(g.shape))
        offset += n
    moments_old = (moment_qkv, moment_out, moment_up, moment_down)
    new_moments = []
    nesterov = []
    for which in range(4):
        total = sums[which].astype(jnp.float32)
        fresh = keep_rate * moments_old[which] + total
        new_moments.append(fresh)
        nesterov.append((total + keep_rate * fresh).astype(jnp.bfloat16))

    core = lax.axis_index("dp") % 2
    partner = [(d, d ^ 1) for d in range(replicas)]

    def exchange(value):
        return lax.ppermute(value, "dp", partner)

    shapes = [(p.shape[0] * groups, p.shape[1]) for p in nesterov]
    flipped = [rows > cols for rows, cols in shapes]
    wide_rows = max(min(s) for s in shapes)
    half_cols = max(max(s) for s in shapes) // 2
    halves = []
    for which in range(4):
        part = nesterov[which]
        axis = 0 if flipped[which] else 1
        size = part.shape[axis] // 2
        halves.append(lax.dynamic_slice_in_dim(part, core * size, size, axis))
    slot = max(h.size for h in halves) // lanes
    owners = [which * groups // 4 for which in range(4)]
    owned = jnp.int32(4)
    for which in range(4):
        owned = jnp.where(myself == owners[which], which, owned)

    pieces = [jnp.zeros((slot, lanes), jnp.bfloat16)] * groups
    for which in range(4):
        part = halves[which].reshape(-1, lanes)
        pieces[owners[which]] = jnp.pad(part, ((0, slot - part.shape[0]), (0, 0)))
    outgoing = jnp.stack(pieces)
    incoming = lax.all_to_all(outgoing, "shard", 0, 0, tiled=True)

    def assemble(which):
        hr, hc = halves[which].shape

        def branch(buffer):
            used = hr * hc // lanes
            whole = buffer[:, :used, :].reshape(groups * hr, hc)
            if flipped[which]:
                whole = whole.T
            r, c = whole.shape
            return jnp.pad(whole, ((0, wide_rows - r), (0, half_cols - c)))

        return branch

    def nothing(buffer):
        return jnp.zeros((wide_rows, half_cols), jnp.bfloat16)

    matrix = lax.switch(owned, [assemble(w) for w in range(4)] + [nothing], incoming)
    factors = jnp.array([0.2 * max(s) ** 0.5 for s in shapes] + [0.0], jnp.float32)
    result = newton_schulz(matrix, factors[owned], exchange)

    def disassemble(which):
        hr, hc = halves[which].shape

        def branch(y):
            if flipped[which]:
                part = y[:hc, : groups * hr].T
            else:
                part = y[: groups * hr, :hc]
            part = part.reshape(groups, -1, lanes)
            return jnp.pad(part, ((0, 0), (0, slot - part.shape[1]), (0, 0)))

        return branch

    def nothing_back(y):
        return jnp.zeros((groups, slot, lanes), jnp.bfloat16)

    answered = lax.switch(owned, [disassemble(w) for w in range(4)] + [nothing_back], result)
    returned = lax.all_to_all(answered, "shard", 0, 0, tiled=True)
    mine = jnp.stack([returned[owners[which]] for which in range(4)])
    theirs = exchange(mine)
    first = core == 0
    updates = []
    for which in range(4):
        hr, hc = halves[which].shape
        used = hr * hc // lanes
        own = mine[which, :used].reshape(hr, hc)
        other = theirs[which, :used].reshape(hr, hc)
        low = jnp.where(first, own, other)
        high = jnp.where(first, other, own)
        updates.append(jnp.concatenate([low, high], axis=0 if flipped[which] else 1))

    _, grad_embed = lax.optimization_barrier((incoming, grad_embed))
    embed_total = lax.psum_scatter(grad_embed, "dp", scatter_dimension=1, tiled=True).astype(
        jnp.float32
    )
    embed_new = adamw(embed_total, embed_param, embed_first, embed_second)
    bias_new = adamw(sums[4].astype(jnp.float32), bias_param, bias_first, bias_second)
    return (
        new_moments[0],
        updates[0],
        new_moments[1],
        updates[1],
        new_moments[2],
        updates[2],
        new_moments[3],
        updates[3],
        embed_new[0],
        embed_new[1],
        embed_new[2],
        bias_new[0],
        bias_new[1],
        bias_new[2],
    )


def solution(mesh):
    placed = (
        P("dp", "shard", None),
        P("dp", "shard", None),
        P("dp", "shard", None),
        P("dp", "shard", None),
        P("dp", None),
        P("dp", "shard", None),
        P("shard", None),
        P("shard", None),
        P("shard", None),
        P("shard", None),
        P("shard", "dp", None),
        P("shard", "dp", None),
        P("shard", "dp", None),
        P(),
        P(),
        P(),
    )
    return jax.shard_map(
        local,
        mesh=mesh,
        in_specs=placed,
        out_specs=(
            P("shard", None),
            P("shard", None),
            P("shard", None),
            P("shard", None),
            P("shard", None),
            P("shard", None),
            P("shard", None),
            P("shard", None),
            P("shard", "dp", None),
            P("shard", "dp", None),
            P("shard", "dp", None),
            P(),
            P(),
            P(),
        ),
        check_vma=False,
    )
```

```python
import jax
import jax.numpy as jnp
from jax import lax
from jax.sharding import PartitionSpec as P

ITERS = 3
STEP = 10


coef_a = 3.4445
coef_b = -4.775
coef_c = 2.0315
keep_rate = 0.95
beta_one = 0.9
beta_two = 0.999
learn_rate = 0.001
decay_rate = 0.01
adam_eps = 1e-08


def newton_schulz(current, factor, exchange):
    wide = current.astype(jnp.float32)
    squares = jnp.sum(wide * wide)
    norm_value = jnp.sqrt(squares + exchange(squares))
    current = (wide / (norm_value + 1e-07)).astype(jnp.bfloat16)
    result = current
    for turn in range(ITERS):
        part = jnp.dot(current, current.T, preferred_element_type=jnp.bfloat16)
        gram = (part.astype(jnp.float32) + exchange(part).astype(jnp.float32)).astype(jnp.bfloat16)
        square = jnp.dot(gram, gram, preferred_element_type=jnp.float32)
        poly = (coef_b * gram.astype(jnp.float32) + coef_c * square).astype(jnp.bfloat16)
        following = coef_a * current.astype(jnp.float32) + jnp.dot(
            poly, current, preferred_element_type=jnp.float32
        )
        if turn + 1 < ITERS:
            current = following.astype(jnp.bfloat16)
        else:
            result = (factor * following).astype(jnp.bfloat16)
    return result


def adamw(total, param, first, second):
    first_new = beta_one * first + (1.0 - beta_one) * total
    second_new = beta_two * second + (1.0 - beta_two) * total * total
    first_hat = first_new / (1.0 - beta_one**STEP)
    second_hat = second_new / (1.0 - beta_two**STEP)
    param_new = param - learn_rate * (
        first_hat / (jnp.sqrt(second_hat) + adam_eps) + decay_rate * param
    )
    return (param_new, first_new, second_new)


def local(
    grad_qkv,
    grad_out,
    grad_up,
    grad_down,
    grad_bias,
    grad_embed,
    moment_qkv,
    moment_out,
    moment_up,
    moment_down,
    embed_param,
    embed_first,
    embed_second,
    bias_param,
    bias_first,
    bias_second,
):
    groups = lax.axis_size("shard")
    replicas = lax.axis_size("dp")
    myself = lax.axis_index("shard")
    lanes = 128
    grads = (grad_qkv[0], grad_out[0], grad_up[0], grad_down[0], grad_bias[0])
    sizes = [g.size for g in grads]
    flat = jnp.concatenate([g.reshape(-1) for g in grads])
    block = replicas * 16 * lanes
    padded = -(-flat.shape[0] // block) * block
    flat = jnp.pad(flat, (0, padded - flat.shape[0])).reshape(padded // lanes, lanes)
    parts = lax.all_to_all(flat.reshape(replicas, -1, lanes), "dp", 0, 0, tiled=True)
    reduced = jnp.sum(parts.astype(jnp.float32), axis=0).astype(jnp.bfloat16)
    gathered = lax.all_gather(reduced, "dp", axis=0, tiled=True).reshape(-1)
    sums = []
    offset = 0
    for g, n in zip(grads, sizes):
        sums.append(gathered[offset : offset + n].reshape(g.shape))
        offset += n
    moments_old = (moment_qkv, moment_out, moment_up, moment_down)
    new_moments = []
    nesterov = []
    for which in range(4):
        total = sums[which].astype(jnp.float32)
        fresh = keep_rate * moments_old[which] + total
        new_moments.append(fresh)
        nesterov.append((total + keep_rate * fresh).astype(jnp.bfloat16))

    core = lax.axis_index("dp") % 2
    partner = [(d, d ^ 1) for d in range(replicas)]

    def exchange(value):
        return lax.ppermute(value, "dp", partner)

    shapes = [(p.shape[0] * groups, p.shape[1]) for p in nesterov]
    flipped = [rows > cols for rows, cols in shapes]
    wide_rows = max(min(s) for s in shapes)
    half_cols = max(max(s) for s in shapes) // 2
    halves = []
    for which in range(4):
        part = nesterov[which]
        axis = 0 if flipped[which] else 1
        size = part.shape[axis] // 2
        halves.append(lax.dynamic_slice_in_dim(part, core * size, size, axis))
    slot = max(h.size for h in halves) // lanes
    owners = [which * groups // 4 for which in range(4)]
    owned = jnp.int32(4)
    for which in range(4):
        owned = jnp.where(myself == owners[which], which, owned)

    pieces = [jnp.zeros((slot, lanes), jnp.bfloat16)] * groups
    for which in range(4):
        part = halves[which].reshape(-1, lanes)
        pieces[owners[which]] = jnp.pad(part, ((0, slot - part.shape[0]), (0, 0)))
    outgoing = jnp.stack(pieces)
    incoming = lax.all_to_all(outgoing, "shard", 0, 0, tiled=True)

    def assemble(which):
        hr, hc = halves[which].shape

        def branch(buffer):
            used = hr * hc // lanes
            whole = buffer[:, :used, :].reshape(groups * hr, hc)
            if flipped[which]:
                whole = whole.T
            r, c = whole.shape
            return jnp.pad(whole, ((0, wide_rows - r), (0, half_cols - c)))

        return branch

    def nothing(buffer):
        return jnp.zeros((wide_rows, half_cols), jnp.bfloat16)

    matrix = lax.switch(owned, [assemble(w) for w in range(4)] + [nothing], incoming)
    factors = jnp.array([0.2 * max(s) ** 0.5 for s in shapes] + [0.0], jnp.float32)
    result = newton_schulz(matrix, factors[owned], exchange)

    def disassemble(which):
        hr, hc = halves[which].shape

        def branch(y):
            if flipped[which]:
                part = y[:hc, : groups * hr].T
            else:
                part = y[: groups * hr, :hc]
            part = part.reshape(groups, -1, lanes)
            return jnp.pad(part, ((0, 0), (0, slot - part.shape[1]), (0, 0)))

        return branch

    def nothing_back(y):
        return jnp.zeros((groups, slot, lanes), jnp.bfloat16)

    answered = lax.switch(owned, [disassemble(w) for w in range(4)] + [nothing_back], result)
    returned = lax.all_to_all(answered, "shard", 0, 0, tiled=True)
    mine = jnp.stack([returned[owners[which]] for which in range(4)])
    theirs = exchange(mine)
    updates = []
    for which in range(4):
        hr, hc = halves[which].shape
        used = hr * hc // lanes
        axis = 0 if flipped[which] else 1
        size = (hr, hc)[axis]
        own = mine[which, :used].reshape(hr, hc)
        other = theirs[which, :used].reshape(hr, hc)
        whole = jnp.zeros(nesterov[which].shape, jnp.bfloat16)
        whole = lax.dynamic_update_slice_in_dim(whole, own, core * size, axis)
        whole = lax.dynamic_update_slice_in_dim(whole, other, (1 - core) * size, axis)
        updates.append(whole)

    _, grad_embed = lax.optimization_barrier((incoming, grad_embed))
    embed_total = lax.psum_scatter(grad_embed, "dp", scatter_dimension=1, tiled=True).astype(
        jnp.float32
    )
    embed_new = adamw(embed_total, embed_param, embed_first, embed_second)
    bias_new = adamw(sums[4].astype(jnp.float32), bias_param, bias_first, bias_second)
    return (
        new_moments[0],
        updates[0],
        new_moments[1],
        updates[1],
        new_moments[2],
        updates[2],
        new_moments[3],
        updates[3],
        embed_new[0],
        embed_new[1],
        embed_new[2],
        bias_new[0],
        bias_new[1],
        bias_new[2],
    )


def solution(mesh):
    placed = (
        P("dp", "shard", None),
        P("dp", "shard", None),
        P("dp", "shard", None),
        P("dp", "shard", None),
        P("dp", None),
        P("dp", "shard", None),
        P("shard", None),
        P("shard", None),
        P("shard", None),
        P("shard", None),
        P("shard", "dp", None),
        P("shard", "dp", None),
        P("shard", "dp", None),
        P(),
        P(),
        P(),
    )
    return jax.shard_map(
        local,
        mesh=mesh,
        in_specs=placed,
        out_specs=(
            P("shard", None),
            P("shard", None),
            P("shard", None),
            P("shard", None),
            P("shard", None),
            P("shard", None),
            P("shard", None),
            P("shard", None),
            P("shard", "dp", None),
            P("shard", "dp", None),
            P("shard", "dp", None),
            P(),
            P(),
            P(),
        ),
        check_vma=False,
    )
```

```python
import jax
import jax.numpy as jnp
from jax import lax
from jax.sharding import PartitionSpec as P

ITERS = 3
STEP = 10


coef_a = 3.4445
coef_b = -4.775
coef_c = 2.0315
keep_rate = 0.95
beta_one = 0.9
beta_two = 0.999
learn_rate = 0.001
decay_rate = 0.01
adam_eps = 1e-08


def newton_schulz(current, factor, exchange):
    wide = current.astype(jnp.float32)
    squares = jnp.sum(wide * wide)
    norm_value = jnp.sqrt(squares + exchange(squares))
    current = (wide / (norm_value + 1e-07)).astype(jnp.bfloat16)
    result = current
    for turn in range(ITERS):
        part = jnp.dot(current, current.T, preferred_element_type=jnp.bfloat16)
        gram = (part.astype(jnp.float32) + exchange(part).astype(jnp.float32)).astype(jnp.bfloat16)
        square = jnp.dot(gram, gram, preferred_element_type=jnp.float32)
        poly = (coef_b * gram.astype(jnp.float32) + coef_c * square).astype(jnp.bfloat16)
        following = coef_a * current.astype(jnp.float32) + jnp.dot(
            poly, current, preferred_element_type=jnp.float32
        )
        if turn + 1 < ITERS:
            current = following.astype(jnp.bfloat16)
        else:
            result = (factor * following).astype(jnp.bfloat16)
    return result


def adamw(total, param, first, second):
    first_new = beta_one * first + (1.0 - beta_one) * total
    second_new = beta_two * second + (1.0 - beta_two) * total * total
    first_hat = first_new / (1.0 - beta_one**STEP)
    second_hat = second_new / (1.0 - beta_two**STEP)
    param_new = param - learn_rate * (
        first_hat / (jnp.sqrt(second_hat) + adam_eps) + decay_rate * param
    )
    return (param_new, first_new, second_new)


def local(
    grad_qkv,
    grad_out,
    grad_up,
    grad_down,
    grad_bias,
    grad_embed,
    moment_qkv,
    moment_out,
    moment_up,
    moment_down,
    embed_param,
    embed_first,
    embed_second,
    bias_param,
    bias_first,
    bias_second,
):
    groups = lax.axis_size("shard")
    replicas = lax.axis_size("dp")
    myself = lax.axis_index("shard")
    lanes = 128
    grads = (grad_qkv[0], grad_out[0], grad_up[0], grad_down[0], grad_bias[0])
    sizes = [g.size for g in grads]
    flat = jnp.concatenate([g.reshape(-1) for g in grads])
    block = replicas * 16 * lanes
    padded = -(-flat.shape[0] // block) * block
    flat = jnp.pad(flat, (0, padded - flat.shape[0])).reshape(padded // lanes, lanes)
    parts = lax.all_to_all(flat.reshape(replicas, -1, lanes), "dp", 0, 0, tiled=True)
    reduced = jnp.sum(parts.astype(jnp.float32), axis=0).astype(jnp.bfloat16)
    gathered = lax.all_gather(reduced, "dp", axis=0, tiled=True).reshape(-1)
    sums = []
    offset = 0
    for g, n in zip(grads, sizes):
        sums.append(gathered[offset : offset + n].reshape(g.shape))
        offset += n
    moments_old = (moment_qkv, moment_out, moment_up, moment_down)
    new_moments = []
    nesterov = []
    for which in range(4):
        total = sums[which].astype(jnp.float32)
        fresh = keep_rate * moments_old[which] + total
        new_moments.append(fresh)
        nesterov.append((total + keep_rate * fresh).astype(jnp.bfloat16))

    core = lax.axis_index("dp") % 2
    partner = [(d, d ^ 1) for d in range(replicas)]

    def exchange(value):
        return lax.ppermute(value, "dp", partner)

    shapes = [(p.shape[0] * groups, p.shape[1]) for p in nesterov]
    flipped = [rows > cols for rows, cols in shapes]
    wide_rows = max(min(s) for s in shapes)
    half_cols = max(max(s) for s in shapes) // 2
    halves = []
    for which in range(4):
        part = nesterov[which]
        axis = 0 if flipped[which] else 1
        size = part.shape[axis] // 2
        halves.append(lax.dynamic_slice_in_dim(part, core * size, size, axis))
    slot = max(h.size for h in halves) // lanes
    owners = [which * groups // 4 for which in range(4)]
    owned = jnp.int32(4)
    for which in range(4):
        owned = jnp.where(myself == owners[which], which, owned)

    outgoing = jnp.zeros((groups, slot, lanes), jnp.bfloat16)
    for which in range(4):
        part = halves[which].reshape(1, -1, lanes)
        outgoing = lax.dynamic_update_slice(outgoing, part, (owners[which], 0, 0))
    incoming = lax.all_to_all(outgoing, "shard", 0, 0, tiled=True)

    def assemble(which):
        hr, hc = halves[which].shape

        def branch(buffer):
            used = hr * hc // lanes
            whole = buffer[:, :used, :].reshape(groups * hr, hc)
            if flipped[which]:
                whole = whole.T
            r, c = whole.shape
            return jnp.pad(whole, ((0, wide_rows - r), (0, half_cols - c)))

        return branch

    def nothing(buffer):
        return jnp.zeros((wide_rows, half_cols), jnp.bfloat16)

    matrix = lax.switch(owned, [assemble(w) for w in range(4)] + [nothing], incoming)
    factors = jnp.array([0.2 * max(s) ** 0.5 for s in shapes] + [0.0], jnp.float32)
    result = newton_schulz(matrix, factors[owned], exchange)

    def disassemble(which):
        hr, hc = halves[which].shape

        def branch(y):
            if flipped[which]:
                part = y[:hc, : groups * hr].T
            else:
                part = y[: groups * hr, :hc]
            part = part.reshape(groups, -1, lanes)
            empty = jnp.zeros((groups, slot, lanes), jnp.bfloat16)
            return lax.dynamic_update_slice(empty, part, (0, 0, 0))

        return branch

    def nothing_back(y):
        return jnp.zeros((groups, slot, lanes), jnp.bfloat16)

    answered = lax.switch(owned, [disassemble(w) for w in range(4)] + [nothing_back], result)
    returned = lax.all_to_all(answered, "shard", 0, 0, tiled=True)
    mine = jnp.stack([returned[owners[which]] for which in range(4)])
    theirs = exchange(mine)
    updates = []
    for which in range(4):
        hr, hc = halves[which].shape
        used = hr * hc // lanes
        axis = 0 if flipped[which] else 1
        size = (hr, hc)[axis]
        own = mine[which, :used].reshape(hr, hc)
        other = theirs[which, :used].reshape(hr, hc)
        whole = jnp.zeros(nesterov[which].shape, jnp.bfloat16)
        whole = lax.dynamic_update_slice_in_dim(whole, own, core * size, axis)
        whole = lax.dynamic_update_slice_in_dim(whole, other, (1 - core) * size, axis)
        updates.append(whole)

    _, grad_embed = lax.optimization_barrier((incoming, grad_embed))
    embed_total = lax.psum_scatter(grad_embed, "dp", scatter_dimension=1, tiled=True).astype(
        jnp.float32
    )
    embed_new = adamw(embed_total, embed_param, embed_first, embed_second)
    bias_new = adamw(sums[4].astype(jnp.float32), bias_param, bias_first, bias_second)
    return (
        new_moments[0],
        updates[0],
        new_moments[1],
        updates[1],
        new_moments[2],
        updates[2],
        new_moments[3],
        updates[3],
        embed_new[0],
        embed_new[1],
        embed_new[2],
        bias_new[0],
        bias_new[1],
        bias_new[2],
    )


def solution(mesh):
    placed = (
        P("dp", "shard", None),
        P("dp", "shard", None),
        P("dp", "shard", None),
        P("dp", "shard", None),
        P("dp", None),
        P("dp", "shard", None),
        P("shard", None),
        P("shard", None),
        P("shard", None),
        P("shard", None),
        P("shard", "dp", None),
        P("shard", "dp", None),
        P("shard", "dp", None),
        P(),
        P(),
        P(),
    )
    return jax.shard_map(
        local,
        mesh=mesh,
        in_specs=placed,
        out_specs=(
            P("shard", None),
            P("shard", None),
            P("shard", None),
            P("shard", None),
            P("shard", None),
            P("shard", None),
            P("shard", None),
            P("shard", None),
            P("shard", "dp", None),
            P("shard", "dp", None),
            P("shard", "dp", None),
            P(),
            P(),
            P(),
        ),
        check_vma=False,
    )
```

```python
import jax
import jax.numpy as jnp
from jax import lax
from jax.sharding import PartitionSpec as P

ITERS = 3
STEP = 10


coef_a = 3.4445
coef_b = -4.775
coef_c = 2.0315
keep_rate = 0.95
beta_one = 0.9
beta_two = 0.999
learn_rate = 0.001
decay_rate = 0.01
adam_eps = 1e-08


def newton_schulz(current, factor, exchange):
    wide = current.astype(jnp.float32)
    squares = jnp.sum(wide * wide)
    norm_value = jnp.sqrt(squares + exchange(squares))
    current = (wide / (norm_value + 1e-07)).astype(jnp.bfloat16)
    result = current
    for turn in range(ITERS):
        part = jnp.dot(current, current.T, preferred_element_type=jnp.bfloat16)
        gram = (part.astype(jnp.float32) + exchange(part).astype(jnp.float32)).astype(jnp.bfloat16)
        square = jnp.dot(gram, gram, preferred_element_type=jnp.float32)
        poly = (coef_b * gram.astype(jnp.float32) + coef_c * square).astype(jnp.bfloat16)
        following = coef_a * current.astype(jnp.float32) + jnp.dot(
            poly, current, preferred_element_type=jnp.float32
        )
        if turn + 1 < ITERS:
            current = following.astype(jnp.bfloat16)
        else:
            result = (factor * following).astype(jnp.bfloat16)
    return result


def adamw(total, param, first, second):
    first_new = beta_one * first + (1.0 - beta_one) * total
    second_new = beta_two * second + (1.0 - beta_two) * total * total
    first_hat = first_new / (1.0 - beta_one**STEP)
    second_hat = second_new / (1.0 - beta_two**STEP)
    param_new = param - learn_rate * (
        first_hat / (jnp.sqrt(second_hat) + adam_eps) + decay_rate * param
    )
    return (param_new, first_new, second_new)


def local(
    grad_qkv,
    grad_out,
    grad_up,
    grad_down,
    grad_bias,
    grad_embed,
    moment_qkv,
    moment_out,
    moment_up,
    moment_down,
    embed_param,
    embed_first,
    embed_second,
    bias_param,
    bias_first,
    bias_second,
):
    groups = lax.axis_size("shard")
    replicas = lax.axis_size("dp")
    myself = lax.axis_index("shard")
    lanes = 128
    grads = (grad_qkv[0], grad_out[0], grad_up[0], grad_down[0], grad_bias[0])
    sizes = [g.size for g in grads]
    flat = jnp.concatenate([g.reshape(-1) for g in grads])
    block = replicas * 16 * lanes
    padded = -(-flat.shape[0] // block) * block
    flat = jnp.pad(flat, (0, padded - flat.shape[0])).reshape(padded // lanes, lanes)
    blocks = flat.reshape(replicas, -1, lanes)
    split = blocks.shape[1] // 2
    collected = []
    for rows in (slice(0, split), slice(split, None)):
        parts = lax.all_to_all(blocks[:, rows, :], "dp", 0, 0, tiled=True)
        reduced = jnp.sum(parts.astype(jnp.float32), axis=0).astype(jnp.bfloat16)
        collected.append(lax.all_gather(reduced, "dp", axis=0, tiled=False))
    gathered = jnp.concatenate(collected, axis=1).reshape(-1)
    sums = []
    offset = 0
    for g, n in zip(grads, sizes):
        sums.append(gathered[offset : offset + n].reshape(g.shape))
        offset += n
    moments_old = (moment_qkv, moment_out, moment_up, moment_down)
    new_moments = []
    nesterov = []
    for which in range(4):
        total = sums[which].astype(jnp.float32)
        fresh = keep_rate * moments_old[which] + total
        new_moments.append(fresh)
        nesterov.append((total + keep_rate * fresh).astype(jnp.bfloat16))

    core = lax.axis_index("dp") % 2
    partner = [(d, d ^ 1) for d in range(replicas)]

    def exchange(value):
        return lax.ppermute(value, "dp", partner)

    shapes = [(p.shape[0] * groups, p.shape[1]) for p in nesterov]
    flipped = [rows > cols for rows, cols in shapes]
    wide_rows = max(min(s) for s in shapes)
    half_cols = max(max(s) for s in shapes) // 2
    halves = []
    for which in range(4):
        part = nesterov[which]
        axis = 0 if flipped[which] else 1
        size = part.shape[axis] // 2
        halves.append(lax.dynamic_slice_in_dim(part, core * size, size, axis))
    slot = max(h.size for h in halves) // lanes
    owners = [which * groups // 4 for which in range(4)]
    owned = jnp.int32(4)
    for which in range(4):
        owned = jnp.where(myself == owners[which], which, owned)

    outgoing = jnp.zeros((groups, slot, lanes), jnp.bfloat16)
    for which in range(4):
        part = halves[which].reshape(1, -1, lanes)
        outgoing = lax.dynamic_update_slice(outgoing, part, (owners[which], 0, 0))
    incoming = lax.all_to_all(outgoing, "shard", 0, 0, tiled=True)

    def assemble(which):
        hr, hc = halves[which].shape

        def branch(buffer):
            used = hr * hc // lanes
            whole = buffer[:, :used, :].reshape(groups * hr, hc)
            if flipped[which]:
                whole = whole.T
            r, c = whole.shape
            return jnp.pad(whole, ((0, wide_rows - r), (0, half_cols - c)))

        return branch

    def nothing(buffer):
        return jnp.zeros((wide_rows, half_cols), jnp.bfloat16)

    matrix = lax.switch(owned, [assemble(w) for w in range(4)] + [nothing], incoming)
    factors = jnp.array([0.2 * max(s) ** 0.5 for s in shapes] + [0.0], jnp.float32)
    result = newton_schulz(matrix, factors[owned], exchange)

    def disassemble(which):
        hr, hc = halves[which].shape

        def branch(y):
            if flipped[which]:
                part = y[:hc, : groups * hr].T
            else:
                part = y[: groups * hr, :hc]
            part = part.reshape(groups, -1, lanes)
            empty = jnp.zeros((groups, slot, lanes), jnp.bfloat16)
            return lax.dynamic_update_slice(empty, part, (0, 0, 0))

        return branch

    def nothing_back(y):
        return jnp.zeros((groups, slot, lanes), jnp.bfloat16)

    answered = lax.switch(owned, [disassemble(w) for w in range(4)] + [nothing_back], result)
    returned = lax.all_to_all(answered, "shard", 0, 0, tiled=True)
    mine = jnp.stack([returned[owners[which]] for which in range(4)])
    theirs = exchange(mine)
    updates = []
    for which in range(4):
        hr, hc = halves[which].shape
        used = hr * hc // lanes
        axis = 0 if flipped[which] else 1
        size = (hr, hc)[axis]
        own = mine[which, :used].reshape(hr, hc)
        other = theirs[which, :used].reshape(hr, hc)
        whole = jnp.zeros(nesterov[which].shape, jnp.bfloat16)
        whole = lax.dynamic_update_slice_in_dim(whole, own, core * size, axis)
        whole = lax.dynamic_update_slice_in_dim(whole, other, (1 - core) * size, axis)
        updates.append(whole)

    _, grad_embed = lax.optimization_barrier((incoming, grad_embed))
    embed_total = lax.psum_scatter(grad_embed, "dp", scatter_dimension=1, tiled=True).astype(
        jnp.float32
    )
    embed_new = adamw(embed_total, embed_param, embed_first, embed_second)
    bias_new = adamw(sums[4].astype(jnp.float32), bias_param, bias_first, bias_second)
    return (
        new_moments[0],
        updates[0],
        new_moments[1],
        updates[1],
        new_moments[2],
        updates[2],
        new_moments[3],
        updates[3],
        embed_new[0],
        embed_new[1],
        embed_new[2],
        bias_new[0],
        bias_new[1],
        bias_new[2],
    )


def solution(mesh):
    placed = (
        P("dp", "shard", None),
        P("dp", "shard", None),
        P("dp", "shard", None),
        P("dp", "shard", None),
        P("dp", None),
        P("dp", "shard", None),
        P("shard", None),
        P("shard", None),
        P("shard", None),
        P("shard", None),
        P("shard", "dp", None),
        P("shard", "dp", None),
        P("shard", "dp", None),
        P(),
        P(),
        P(),
    )
    return jax.shard_map(
        local,
        mesh=mesh,
        in_specs=placed,
        out_specs=(
            P("shard", None),
            P("shard", None),
            P("shard", None),
            P("shard", None),
            P("shard", None),
            P("shard", None),
            P("shard", None),
            P("shard", None),
            P("shard", "dp", None),
            P("shard", "dp", None),
            P("shard", "dp", None),
            P(),
            P(),
            P(),
        ),
        check_vma=False,
    )
```

```python
import jax
import jax.numpy as jnp
from jax import lax
from jax.sharding import PartitionSpec as P

ITERS = 3
STEP = 10


coef_a = 3.4445
coef_b = -4.775
coef_c = 2.0315
keep_rate = 0.95
beta_one = 0.9
beta_two = 0.999
learn_rate = 0.001
decay_rate = 0.01
adam_eps = 1e-08


def newton_schulz(current, factor, exchange):
    wide = current.astype(jnp.float32)
    squares = jnp.sum(wide * wide)
    norm_value = jnp.sqrt(squares + exchange(squares))
    current = (wide / (norm_value + 1e-07)).astype(jnp.bfloat16)
    result = current
    for turn in range(ITERS):
        part = jnp.dot(current, current.T, preferred_element_type=jnp.bfloat16)
        gram = (part.astype(jnp.float32) + exchange(part).astype(jnp.float32)).astype(jnp.bfloat16)
        square = jnp.dot(gram, gram, preferred_element_type=jnp.float32)
        poly = (coef_b * gram.astype(jnp.float32) + coef_c * square).astype(jnp.bfloat16)
        following = coef_a * current.astype(jnp.float32) + jnp.dot(
            poly, current, preferred_element_type=jnp.float32
        )
        if turn + 1 < ITERS:
            current = following.astype(jnp.bfloat16)
        else:
            result = (factor * following).astype(jnp.bfloat16)
    return result


def adamw(total, param, first, second):
    first_new = beta_one * first + (1.0 - beta_one) * total
    second_new = beta_two * second + (1.0 - beta_two) * total * total
    first_hat = first_new / (1.0 - beta_one**STEP)
    second_hat = second_new / (1.0 - beta_two**STEP)
    param_new = param - learn_rate * (
        first_hat / (jnp.sqrt(second_hat) + adam_eps) + decay_rate * param
    )
    return (param_new, first_new, second_new)


def local(
    grad_qkv,
    grad_out,
    grad_up,
    grad_down,
    grad_bias,
    grad_embed,
    moment_qkv,
    moment_out,
    moment_up,
    moment_down,
    embed_param,
    embed_first,
    embed_second,
    bias_param,
    bias_first,
    bias_second,
):
    groups = lax.axis_size("shard")
    replicas = lax.axis_size("dp")
    myself = lax.axis_index("shard")
    lanes = 128
    grads = (grad_qkv[0], grad_out[0], grad_up[0], grad_down[0], grad_bias[0])
    sizes = [g.size for g in grads]
    flat = jnp.concatenate([g.reshape(-1) for g in grads])
    block = replicas * 16 * lanes
    padded = -(-flat.shape[0] // block) * block
    flat = jnp.pad(flat, (0, padded - flat.shape[0])).reshape(padded // lanes, lanes)
    parts = lax.all_to_all(flat.reshape(replicas, -1, lanes), "dp", 0, 0, tiled=True)
    reduced = jnp.sum(parts.astype(jnp.float32), axis=0).astype(jnp.bfloat16)
    gathered = lax.all_gather(reduced, "dp", axis=0, tiled=True).reshape(-1)
    sums = []
    offset = 0
    for g, n in zip(grads, sizes):
        sums.append(gathered[offset : offset + n].reshape(g.shape))
        offset += n
    moments_old = (moment_qkv, moment_out, moment_up, moment_down)
    nesterov = []
    for which in range(4):
        total = sums[which].astype(jnp.float32)
        fresh = keep_rate * moments_old[which] + total
        nesterov.append((total + keep_rate * fresh).astype(jnp.bfloat16))

    core = lax.axis_index("dp") % 2
    partner = [(d, d ^ 1) for d in range(replicas)]

    def exchange(value):
        return lax.ppermute(value, "dp", partner)

    shapes = [(p.shape[0] * groups, p.shape[1]) for p in nesterov]
    flipped = [rows > cols for rows, cols in shapes]
    wide_rows = max(min(s) for s in shapes)
    half_cols = max(max(s) for s in shapes) // 2
    halves = []
    for which in range(4):
        part = nesterov[which]
        axis = 0 if flipped[which] else 1
        size = part.shape[axis] // 2
        halves.append(lax.dynamic_slice_in_dim(part, core * size, size, axis))
    slot = max(h.size for h in halves) // lanes
    owners = [which * groups // 4 for which in range(4)]
    owned = jnp.int32(4)
    for which in range(4):
        owned = jnp.where(myself == owners[which], which, owned)

    outgoing = jnp.zeros((groups, slot, lanes), jnp.bfloat16)
    for which in range(4):
        part = halves[which].reshape(1, -1, lanes)
        outgoing = lax.dynamic_update_slice(outgoing, part, (owners[which], 0, 0))
    incoming = lax.all_to_all(outgoing, "shard", 0, 0, tiled=True)
    _, late_moments = lax.optimization_barrier((outgoing, moments_old))
    new_moments = [
        keep_rate * late_moments[which] + sums[which].astype(jnp.float32) for which in range(4)
    ]

    def assemble(which):
        hr, hc = halves[which].shape

        def branch(buffer):
            used = hr * hc // lanes
            whole = buffer[:, :used, :].reshape(groups * hr, hc)
            if flipped[which]:
                whole = whole.T
            r, c = whole.shape
            return jnp.pad(whole, ((0, wide_rows - r), (0, half_cols - c)))

        return branch

    def nothing(buffer):
        return jnp.zeros((wide_rows, half_cols), jnp.bfloat16)

    matrix = lax.switch(owned, [assemble(w) for w in range(4)] + [nothing], incoming)
    factors = jnp.array([0.2 * max(s) ** 0.5 for s in shapes] + [0.0], jnp.float32)
    result = newton_schulz(matrix, factors[owned], exchange)

    def disassemble(which):
        hr, hc = halves[which].shape

        def branch(y):
            if flipped[which]:
                part = y[:hc, : groups * hr].T
            else:
                part = y[: groups * hr, :hc]
            part = part.reshape(groups, -1, lanes)
            empty = jnp.zeros((groups, slot, lanes), jnp.bfloat16)
            return lax.dynamic_update_slice(empty, part, (0, 0, 0))

        return branch

    def nothing_back(y):
        return jnp.zeros((groups, slot, lanes), jnp.bfloat16)

    answered = lax.switch(owned, [disassemble(w) for w in range(4)] + [nothing_back], result)
    returned = lax.all_to_all(answered, "shard", 0, 0, tiled=True)
    mine = jnp.stack([returned[owners[which]] for which in range(4)])
    theirs = exchange(mine)
    updates = []
    for which in range(4):
        hr, hc = halves[which].shape
        used = hr * hc // lanes
        axis = 0 if flipped[which] else 1
        size = (hr, hc)[axis]
        own = mine[which, :used].reshape(hr, hc)
        other = theirs[which, :used].reshape(hr, hc)
        whole = jnp.zeros(nesterov[which].shape, jnp.bfloat16)
        whole = lax.dynamic_update_slice_in_dim(whole, own, core * size, axis)
        whole = lax.dynamic_update_slice_in_dim(whole, other, (1 - core) * size, axis)
        updates.append(whole)

    _, grad_embed = lax.optimization_barrier((incoming, grad_embed))
    embed_total = lax.psum_scatter(grad_embed, "dp", scatter_dimension=1, tiled=True).astype(
        jnp.float32
    )
    embed_new = adamw(embed_total, embed_param, embed_first, embed_second)
    bias_new = adamw(sums[4].astype(jnp.float32), bias_param, bias_first, bias_second)
    return (
        new_moments[0],
        updates[0],
        new_moments[1],
        updates[1],
        new_moments[2],
        updates[2],
        new_moments[3],
        updates[3],
        embed_new[0],
        embed_new[1],
        embed_new[2],
        bias_new[0],
        bias_new[1],
        bias_new[2],
    )


def solution(mesh):
    placed = (
        P("dp", "shard", None),
        P("dp", "shard", None),
        P("dp", "shard", None),
        P("dp", "shard", None),
        P("dp", None),
        P("dp", "shard", None),
        P("shard", None),
        P("shard", None),
        P("shard", None),
        P("shard", None),
        P("shard", "dp", None),
        P("shard", "dp", None),
        P("shard", "dp", None),
        P(),
        P(),
        P(),
    )
    return jax.shard_map(
        local,
        mesh=mesh,
        in_specs=placed,
        out_specs=(
            P("shard", None),
            P("shard", None),
            P("shard", None),
            P("shard", None),
            P("shard", None),
            P("shard", None),
            P("shard", None),
            P("shard", None),
            P("shard", "dp", None),
            P("shard", "dp", None),
            P("shard", "dp", None),
            P(),
            P(),
            P(),
        ),
        check_vma=False,
    )
```

```python
import jax
import jax.numpy as jnp
from jax import lax
from jax.sharding import PartitionSpec as P

ITERS = 3
STEP = 10


coef_a = 3.4445
coef_b = -4.775
coef_c = 2.0315
keep_rate = 0.95
beta_one = 0.9
beta_two = 0.999
learn_rate = 0.001
decay_rate = 0.01
adam_eps = 1e-08


def newton_schulz(current, factor, exchange):
    wide = current.astype(jnp.float32)
    squares = jnp.sum(wide * wide)
    norm_value = jnp.sqrt(squares + exchange(squares))
    current = (wide / (norm_value + 1e-07)).astype(jnp.bfloat16)
    result = current
    for turn in range(ITERS):
        part = jnp.dot(current, current.T, preferred_element_type=jnp.bfloat16)
        gram = (part.astype(jnp.float32) + exchange(part).astype(jnp.float32)).astype(jnp.bfloat16)
        square = jnp.dot(gram, gram, preferred_element_type=jnp.float32)
        poly = (coef_b * gram.astype(jnp.float32) + coef_c * square).astype(jnp.bfloat16)
        following = coef_a * current.astype(jnp.float32) + jnp.dot(
            poly, current, preferred_element_type=jnp.float32
        )
        if turn + 1 < ITERS:
            current = following.astype(jnp.bfloat16)
        else:
            result = (factor * following).astype(jnp.bfloat16)
    return result


def adamw(total, param, first, second):
    first_new = beta_one * first + (1.0 - beta_one) * total
    second_new = beta_two * second + (1.0 - beta_two) * total * total
    first_hat = first_new / (1.0 - beta_one**STEP)
    second_hat = second_new / (1.0 - beta_two**STEP)
    param_new = param - learn_rate * (
        first_hat / (jnp.sqrt(second_hat) + adam_eps) + decay_rate * param
    )
    return (param_new, first_new, second_new)


def local(
    grad_qkv,
    grad_out,
    grad_up,
    grad_down,
    grad_bias,
    grad_embed,
    moment_qkv,
    moment_out,
    moment_up,
    moment_down,
    embed_param,
    embed_first,
    embed_second,
    bias_param,
    bias_first,
    bias_second,
):
    groups = lax.axis_size("shard")
    replicas = lax.axis_size("dp")
    myself = lax.axis_index("shard")
    lanes = 128
    grads = (grad_qkv[0], grad_out[0], grad_up[0], grad_down[0], grad_bias[0])
    sizes = [g.size for g in grads]
    flat = jnp.concatenate([g.reshape(-1) for g in grads])
    block = replicas * 16 * lanes
    padded = -(-flat.shape[0] // block) * block
    flat = jnp.pad(flat, (0, padded - flat.shape[0])).reshape(padded // lanes, lanes)
    parts = lax.all_to_all(flat.reshape(replicas, -1, lanes), "dp", 0, 0, tiled=True)
    reduced = jnp.sum(parts.astype(jnp.float32), axis=0).astype(jnp.bfloat16)
    copies = jnp.broadcast_to(reduced[None], (replicas,) + reduced.shape)
    gathered = lax.all_to_all(copies, "dp", 0, 0, tiled=True).reshape(-1)
    sums = []
    offset = 0
    for g, n in zip(grads, sizes):
        sums.append(gathered[offset : offset + n].reshape(g.shape))
        offset += n
    moments_old = (moment_qkv, moment_out, moment_up, moment_down)
    new_moments = []
    nesterov = []
    for which in range(4):
        total = sums[which].astype(jnp.float32)
        fresh = keep_rate * moments_old[which] + total
        new_moments.append(fresh)
        nesterov.append((total + keep_rate * fresh).astype(jnp.bfloat16))

    core = lax.axis_index("dp") % 2
    partner = [(d, d ^ 1) for d in range(replicas)]

    def exchange(value):
        return lax.ppermute(value, "dp", partner)

    shapes = [(p.shape[0] * groups, p.shape[1]) for p in nesterov]
    flipped = [rows > cols for rows, cols in shapes]
    wide_rows = max(min(s) for s in shapes)
    half_cols = max(max(s) for s in shapes) // 2
    halves = []
    for which in range(4):
        part = nesterov[which]
        axis = 0 if flipped[which] else 1
        size = part.shape[axis] // 2
        halves.append(lax.dynamic_slice_in_dim(part, core * size, size, axis))
    slot = max(h.size for h in halves) // lanes
    owners = [which * groups // 4 for which in range(4)]
    owned = jnp.int32(4)
    for which in range(4):
        owned = jnp.where(myself == owners[which], which, owned)

    outgoing = jnp.zeros((groups, slot, lanes), jnp.bfloat16)
    for which in range(4):
        part = halves[which].reshape(1, -1, lanes)
        outgoing = lax.dynamic_update_slice(outgoing, part, (owners[which], 0, 0))
    incoming = lax.all_to_all(outgoing, "shard", 0, 0, tiled=True)

    def assemble(which):
        hr, hc = halves[which].shape

        def branch(buffer):
            used = hr * hc // lanes
            whole = buffer[:, :used, :].reshape(groups * hr, hc)
            if flipped[which]:
                whole = whole.T
            r, c = whole.shape
            return jnp.pad(whole, ((0, wide_rows - r), (0, half_cols - c)))

        return branch

    def nothing(buffer):
        return jnp.zeros((wide_rows, half_cols), jnp.bfloat16)

    matrix = lax.switch(owned, [assemble(w) for w in range(4)] + [nothing], incoming)
    factors = jnp.array([0.2 * max(s) ** 0.5 for s in shapes] + [0.0], jnp.float32)
    result = newton_schulz(matrix, factors[owned], exchange)

    def disassemble(which):
        hr, hc = halves[which].shape

        def branch(y):
            if flipped[which]:
                part = y[:hc, : groups * hr].T
            else:
                part = y[: groups * hr, :hc]
            part = part.reshape(groups, -1, lanes)
            empty = jnp.zeros((groups, slot, lanes), jnp.bfloat16)
            return lax.dynamic_update_slice(empty, part, (0, 0, 0))

        return branch

    def nothing_back(y):
        return jnp.zeros((groups, slot, lanes), jnp.bfloat16)

    answered = lax.switch(owned, [disassemble(w) for w in range(4)] + [nothing_back], result)
    returned = lax.all_to_all(answered, "shard", 0, 0, tiled=True)
    mine = jnp.stack([returned[owners[which]] for which in range(4)])
    theirs = exchange(mine)
    updates = []
    for which in range(4):
        hr, hc = halves[which].shape
        used = hr * hc // lanes
        axis = 0 if flipped[which] else 1
        size = (hr, hc)[axis]
        own = mine[which, :used].reshape(hr, hc)
        other = theirs[which, :used].reshape(hr, hc)
        whole = jnp.zeros(nesterov[which].shape, jnp.bfloat16)
        whole = lax.dynamic_update_slice_in_dim(whole, own, core * size, axis)
        whole = lax.dynamic_update_slice_in_dim(whole, other, (1 - core) * size, axis)
        updates.append(whole)

    _, grad_embed = lax.optimization_barrier((incoming, grad_embed))
    embed_total = lax.psum_scatter(grad_embed, "dp", scatter_dimension=1, tiled=True).astype(
        jnp.float32
    )
    embed_new = adamw(embed_total, embed_param, embed_first, embed_second)
    bias_new = adamw(sums[4].astype(jnp.float32), bias_param, bias_first, bias_second)
    return (
        new_moments[0],
        updates[0],
        new_moments[1],
        updates[1],
        new_moments[2],
        updates[2],
        new_moments[3],
        updates[3],
        embed_new[0],
        embed_new[1],
        embed_new[2],
        bias_new[0],
        bias_new[1],
        bias_new[2],
    )


def solution(mesh):
    placed = (
        P("dp", "shard", None),
        P("dp", "shard", None),
        P("dp", "shard", None),
        P("dp", "shard", None),
        P("dp", None),
        P("dp", "shard", None),
        P("shard", None),
        P("shard", None),
        P("shard", None),
        P("shard", None),
        P("shard", "dp", None),
        P("shard", "dp", None),
        P("shard", "dp", None),
        P(),
        P(),
        P(),
    )
    return jax.shard_map(
        local,
        mesh=mesh,
        in_specs=placed,
        out_specs=(
            P("shard", None),
            P("shard", None),
            P("shard", None),
            P("shard", None),
            P("shard", None),
            P("shard", None),
            P("shard", None),
            P("shard", None),
            P("shard", "dp", None),
            P("shard", "dp", None),
            P("shard", "dp", None),
            P(),
            P(),
            P(),
        ),
        check_vma=False,
    )
```
